256 devices in a mesh: row: 16 (over z, core), col: 4 (over x), inner: 4 (over y).
Axes of the slice: x: 4, y: 4, z: 8, core: 2. Of those that a mesh axis runs over, the one named last changes fastest.
Arguments:
- density: bfloat16 [64, 16, 256, 256], P('row', ('col', 'inner')), may hold values from -1.5 to 1.5, as said below
- block_cols: int32 [64, 16], replicated, may hold values from 0 to 63, as said below
- mixing: float32 [3], replicated, may hold values from 0.02 to 1.5, as said below
Outputs:
- purified: bfloat16 [64, 16, 256, 256], P('row', ('col', 'inner'))
The draws below stay inside these ranges and needn't reach their ends.
Inputs may be any that keep to these rules, and one draw needn't show every extreme that they name: Slot g of block row i names a block row of group g (rows g * 4 to g * 4 + 3); within one group of block rows, slot g names each row of group g once. Slot i // 4 of row i names i itself. The pattern is symmetric: row block_cols[i, g] names i in slot i // 4. It is consistent: block_cols[block_cols[i, t], g] == block_cols[i, g] for all i, t, g. `density`: block (i, g) is the transpose of block (block_cols[i, g], i // 4). `mixing`: element 0 lies in 0.5 to 1.5, elements 1 and 2 in 0.02 to 0.05.
All inputs are finite; a program needn't handle non-finite values.
Results may differ from the reference program's by a relative error of at most 0.007.
Values may be sent and summed in bfloat16 or wider, within the bound.
No kernel may reach another device: no remote copies, remote signals or barrier semaphores. Data moves between devices by JAX's collectives and lax.ppermute only.
A program may use at most 128 MiB of HBM per device.

```python
import jax
import jax.numpy as jnp
from jax import lax

B = 256
K = 16
GS = 4
NB = 64


def pattern(key):
    base = jax.random.fold_in(key, 101)
    keys = jax.random.split(base, K)
    labels = jax.vmap(lambda item: jax.random.permutation(item, GS))(keys).astype(jnp.int32)
    inverse = jnp.argsort(labels, axis=-1, stable=True).astype(jnp.int32)
    group_second = jnp.arange(K, dtype=jnp.int32)[None, :, None]
    mapping = labels[group_second, inverse[:, None, :]]
    table = group_second * GS + mapping
    return jnp.transpose(table, (0, 2, 1)).reshape(K * GS, K).astype(jnp.int32)


def draw_block_cols(key, part):
    return pattern(key)


def draw_density(key, part):
    block_cols = pattern(key)
    noise_key = jax.random.fold_in(key, 202)
    spread = (B * K) ** (-0.25)
    raw = jnp.clip(jax.random.normal(noise_key, (NB, K, B, B), jnp.float32), -5.0, 5.0) * spread
    rows_all = jnp.arange(NB, dtype=jnp.int32)
    own_group = rows_all // GS
    mirror = raw[block_cols, own_group[:, None]]
    density = (raw + jnp.swapaxes(mirror, -1, -2)) * 0.5 ** 0.5
    return density.astype(jnp.bfloat16)


def draw_mixing(key, part):
    mix_key = jax.random.fold_in(key, 303)
    values = jax.random.uniform(mix_key, (3,), jnp.float32, 0.0, 1.0)
    lowers = jnp.array([0.5, 0.02, 0.02], jnp.float32)
    uppers = jnp.array([1.5, 0.05, 0.05], jnp.float32)
    return lowers + values * (uppers - lowers)


def setup_inputs(seed: int = 0) -> dict:
    seeds = jax.random.split(jax.random.key(seed), 4)
    density = draw_density(jax.random.fold_in(seeds[3], 71), 0)
    block_cols = draw_block_cols(jax.random.fold_in(seeds[3], 71), 0)
    mixing = draw_mixing(jax.random.fold_in(seeds[3], 71), 0)
    return dict(density=density, block_cols=block_cols, mixing=mixing)


def multiply(left_blocks, right_blocks, block_cols):
    def one_row(row_number):
        targets = block_cols[row_number]
        gathered = right_blocks[targets].astype(jnp.float32)
        row_left = left_blocks[row_number].astype(jnp.float32)
        return jnp.einsum("tab,tgbc->gac", row_left, gathered, precision=lax.Precision.HIGHEST)
    return lax.map(one_row, jnp.arange(NB, dtype=jnp.int32))


def reference(density, block_cols, mixing):
    square = multiply(density, density, block_cols).astype(jnp.bfloat16)
    rows_all = jnp.arange(NB, dtype=jnp.int32)
    on_diagonal = (block_cols == rows_all[:, None]).astype(jnp.float32)
    identity = jnp.eye(B, dtype=jnp.float32)
    mixer_blocks = (mixing[0] * on_diagonal[:, :, None, None] * identity
                    + mixing[1] * density.astype(jnp.float32)
                    + mixing[2] * square.astype(jnp.float32)).astype(jnp.bfloat16)
    purified = multiply(square, mixer_blocks, block_cols)
    return purified.astype(jnp.bfloat16)
```

```python
import functools

import jax
import jax.numpy as jnp
from jax import lax
from jax.experimental import pallas as pl
from jax.experimental.pallas import tpu as pltpu
from jax.sharding import PartitionSpec as P

AXES = ("row", "col", "inner")
CORES = 2
NC = 4
B = 256
HALF = B // 2


def permutation(sizes, move):
    rows, cols, inners = sizes
    pairs = []
    for row in range(rows):
        for col in range(cols):
            for inner in range(inners):
                z, core = divmod(row, CORES)
                sign = 1 if core == 0 else -1
                dz, dx, dy, flip = move(sign)
                to_row = (z + dz) % (rows // CORES) * CORES + (core + flip) % CORES
                to = (to_row * cols + (col + dx) % cols) * inners + (inner + dy) % inners
                pairs.append(((row * cols + col) * inners + inner, to))
    return pairs


def ordered_kernel(cols_ref, d_ref, t_ref, ta_ref, tb_ref):
    u = lax.axis_index("row")
    for c in range(NC):
        a = cols_ref[c, u] - NC * u
        block = d_ref[a, 0]
        t_ref[c] = block
        ta_ref[c] = block[:HALF]
        tb_ref[c] = block[HALF:]


def ordered_tiles(density, block_cols):
    half = jax.ShapeDtypeStruct((NC, HALF, B), jnp.bfloat16)
    return pl.pallas_call(
        ordered_kernel,
        out_shape=(jax.ShapeDtypeStruct((NC, B, B), jnp.bfloat16), half, half),
        in_specs=[
            pl.BlockSpec(memory_space=pltpu.SMEM),
            pl.BlockSpec(memory_space=pltpu.VMEM),
        ],
        out_specs=(pl.BlockSpec(memory_space=pltpu.VMEM),) * 3,
        name="ordered",
    )(block_cols, density)


def load_panels(c, left, right, lbuf, rbuf, lsem, rsem):
    row = lax.axis_index("row")
    x = lax.axis_index("col")
    y = lax.axis_index("inner")
    zs = lax.axis_size("row") // CORES
    xs = lax.axis_size("col")
    ys = lax.axis_size("inner")
    z = row // CORES
    core = row % CORES
    sign = 1 - 2 * core
    own = [0, -1, -2, -3, -4, 1, 2, 3]
    copies = []
    for side in range(2):
        s = sign if side == 0 else -sign
        k = core if side == 0 else 1 - core
        for i, off in enumerate(own):
            u = lax.rem(z + off * s + zs, zs) * CORES + k
            dst = rbuf.at[c, pl.ds(pl.multiple_of(u * B, B), B), :]
            copies.append(pltpu.make_async_copy(right[side * 8 + i].at[c], dst, rsem.at[c]))
    steps = [0, -1, 1, -2]
    for h in range(2):
        for i, outer in enumerate(steps):
            for j, inner in enumerate(steps):
                if h == 0:
                    gx = lax.rem(x + inner * sign + xs, xs)
                    gy = lax.rem(y + outer * sign + ys, ys)
                else:
                    gx = lax.rem(x + outer * sign + xs, xs)
                    gy = lax.rem(y + inner * sign + ys, ys)
                g = gx * ys + gy
                dst = lbuf.at[c, pl.ds(h * HALF, HALF), pl.ds(pl.multiple_of(g * B, B), B)]
                copies.append(pltpu.make_async_copy(left[h * 4 + i].at[j, c], dst, lsem.at[c]))
    for copy in copies:
        copy.start()


def wait_panels(c, lbuf, rbuf, lsem, rsem):
    pltpu.make_async_copy(lbuf.at[c], lbuf.at[c], lsem.at[c]).wait()
    pltpu.make_async_copy(rbuf.at[c], rbuf.at[c], rsem.at[c]).wait()


def square_kernel(*refs):
    mix_ref = refs[0]
    left, right = refs[1:9], refs[9:25]
    sa_ref, sb_ref, m_ref, lbuf, rbuf, lsem, rsem = refs[25:]
    for c in range(NC):
        load_panels(c, left, right, lbuf, rbuf, lsem, rsem)
    u = lax.axis_index("row")
    g = lax.axis_index("col") * lax.axis_size("inner") + lax.axis_index("inner")
    weight = jnp.where(u == g, mix_ref[0], 0.0)
    eye = lax.broadcasted_iota(jnp.int32, (B, B), 0) == lax.broadcasted_iota(jnp.int32, (B, B), 1)
    identity = jnp.where(eye, weight, 0.0)
    for c in range(NC):
        wait_panels(c, lbuf, rbuf, lsem, rsem)
        square = jnp.dot(lbuf[c], rbuf[c], preferred_element_type=jnp.float32).astype(jnp.bfloat16)
        sa_ref[c] = square[:HALF]
        sb_ref[c] = square[HALF:]
        block = rbuf[c, pl.ds(pl.multiple_of(u * B, B), B), :]
        m_ref[c] = (
            identity
            + mix_ref[1] * block.astype(jnp.float32)
            + mix_ref[2] * square.astype(jnp.float32)
        ).astype(jnp.bfloat16)


def purify_kernel(*refs):
    cols_ref = refs[0]
    left, right = refs[1:9], refs[9:25]
    out_ref, lbuf, rbuf, lsem, rsem = refs[25:]
    for c in range(NC):
        load_panels(c, left, right, lbuf, rbuf, lsem, rsem)
    u = lax.axis_index("row")
    for c in range(NC):
        wait_panels(c, lbuf, rbuf, lsem, rsem)
        a = cols_ref[c, u] - NC * u
        out_ref[a, 0] = jnp.dot(
            lbuf[c], rbuf[c], preferred_element_type=jnp.float32
        ).astype(jnp.bfloat16)


def product(kernel, scalars, left, right, out_shape, name):
    depth = len(right) * B
    return pl.pallas_call(
        kernel,
        out_shape=out_shape,
        in_specs=[pl.BlockSpec(memory_space=pltpu.SMEM)]
        + [pl.BlockSpec(memory_space=pl.ANY)] * (len(left) + len(right)),
        out_specs=jax.tree.map(lambda _: pl.BlockSpec(memory_space=pltpu.VMEM), out_shape),
        scratch_shapes=[
            pltpu.VMEM((NC, B, depth), jnp.bfloat16),
            pltpu.VMEM((NC, depth, B), jnp.bfloat16),
            pltpu.SemaphoreType.DMA((NC,)),
            pltpu.SemaphoreType.DMA((NC,)),
        ],
        cost_estimate=pl.CostEstimate(
            flops=2 * NC * B * depth * B, bytes_accessed=4 * NC * B * depth, transcendentals=0
        ),
        name=name,
    )(scalars, *left, *right)


def solution(mesh):
    sizes = tuple(mesh.shape[a] for a in AXES)
    moves = {
        "za": lambda s: (s, 0, 0, 0),
        "zb": lambda s: (-s, 0, 0, 0),
        "xa": lambda s: (0, s, 0, 0),
        "xb": lambda s: (0, -s, 0, 0),
        "ya": lambda s: (0, 0, s, 0),
        "yb": lambda s: (0, 0, -s, 0),
        "core": lambda s: (0, 0, 0, 1),
    }
    perms = {k: permutation(sizes, m) for k, m in moves.items()}

    def send(value, name):
        return lax.ppermute(value, AXES, perms[name])

    def ring4(tile, axis):
        a1 = send(tile, axis + "a")
        b1 = send(tile, axis + "b")
        return [tile, a1, b1, send(a1, axis + "a")]

    def row_panel(half_a, half_b):
        first = ring4(half_a, "x")
        second = ring4(half_b, "y")
        return ring4(jnp.stack(first), "y") + ring4(jnp.stack(second), "x")

    def column_panel(tile):
        forward, backward = [tile], [tile]
        for _ in range(4):
            forward.append(send(forward[-1], "za"))
        for _ in range(3):
            backward.append(send(backward[-1], "zb"))
        own = forward + backward[1:]
        return own + [send(t, "core") for t in own]

    def body(density, block_cols, mixing):
        tile, half_a, half_b = ordered_tiles(density, block_cols)
        half = jax.ShapeDtypeStruct((NC, HALF, B), jnp.bfloat16)
        full = jax.ShapeDtypeStruct((NC, B, B), jnp.bfloat16)
        square_a, square_b, mixer = product(
            square_kernel,
            mixing,
            row_panel(half_a, half_b),
            column_panel(tile),
            (half, half, full),
            "square",
        )
        return product(
            purify_kernel,
            block_cols,
            row_panel(square_a, square_b),
            column_panel(mixer),
            jax.ShapeDtypeStruct(density.shape, jnp.bfloat16),
            "purify",
        )

    in_specs = (P("row", ("col", "inner"), None, None), P(), P())
    out_specs = P("row", ("col", "inner"), None, None)
    return jax.shard_map(body, mesh=mesh, in_specs=in_specs, out_specs=out_specs, check_vma=False)
```

```python
import jax
import jax.numpy as jnp
from jax import lax
from jax.experimental import pallas as pl
from jax.experimental.pallas import tpu as pltpu
from jax.sharding import PartitionSpec as P


AXES = ("row", "col", "inner")
CORES = 2
NC = 4
PAIR = NC // 2
B = 256
RING8 = (0, -1, -2, -3, -4, 1, 2, 3)
RING4 = (-1, 1, -2)
LINES = 1 + 2 * len(RING4)
LEFTS = LINES + 12
RIGHTS = 2 * len(RING8)


def permutation(sizes, move):
    rows, cols, inners = sizes
    pairs = []
    for row in range(rows):
        for col in range(cols):
            for inner in range(inners):
                z, core = divmod(row, CORES)
                sign = 1 if core == 0 else -1
                dz, dx, dy, flip = move(sign)
                to_row = (z + dz) % (rows // CORES) * CORES + (core + flip) % CORES
                to = (to_row * cols + (col + dx) % cols) * inners + (inner + dy) % inners
                pairs.append(((row * cols + col) * inners + inner, to))
    return pairs


def product_kernel(*refs):
    cols_ref, mix_ref, own_ref = refs[:3]
    left, right = refs[3 : 3 + LEFTS], refs[3 + LEFTS : 3 + LEFTS + RIGHTS]
    s_ref, m_ref, lbuf, lsem = refs[3 + LEFTS + RIGHTS :]
    row = lax.axis_index("row")
    x = lax.axis_index("col")
    y = lax.axis_index("inner")
    zs = lax.axis_size("row") // CORES
    xs = lax.axis_size("col")
    ys = lax.axis_size("inner")
    z = row // CORES
    core = row % CORES
    sign = 1 - 2 * core
    weight = jnp.where(row == x * ys + y, mix_ref[0], 0.0)

    def local(c, u):
        return cols_ref[c, u] - NC * u

    @pl.loop(0, NC)
    def _(c):
        a = local(c, row)

        def place(src, dx, dy):
            g = lax.rem(x + dx * sign + xs, xs) * ys + lax.rem(y + dy * sign + ys, ys)
            pltpu.make_async_copy(src, lbuf.at[c, g], lsem.at[c]).start()

        place(left[0].at[a], 0, 0)
        for i, off in enumerate(RING4):
            place(left[1 + i].at[a], off, 0)
            place(left[4 + i].at[a], 0, off)

        @pl.when(a < PAIR)
        def _():
            for i, off in enumerate(RING4):
                place(left[7 + i].at[a], RING4[0], off)
                place(left[7 + i].at[PAIR + a], RING4[1], off)
                place(left[13 + i].at[a], RING4[2], off)

        @pl.when(a >= PAIR)
        def _():
            for i, off in enumerate(RING4):
                place(left[10 + i].at[a - PAIR], off, RING4[0])
                place(left[10 + i].at[a], off, RING4[1])
                place(left[16 + i].at[a - PAIR], off, RING4[2])

    @pl.loop(0, NC)
    def _(c):
        pltpu.make_async_copy(lbuf.at[c], lbuf.at[c], lsem.at[c]).wait()
        total = jnp.zeros((B, B), jnp.float32)
        for side in range(CORES):
            s = sign if side == 0 else -sign
            k = core if side == 0 else 1 - core
            for i, off in enumerate(RING8):
                u = lax.rem(z + off * s + zs, zs) * CORES + k
                total += jnp.dot(
                    lbuf[c, u],
                    right[side * len(RING8) + i][local(c, u)],
                    preferred_element_type=jnp.float32,
                )
        square = total.astype(jnp.bfloat16)
        a = local(c, row)
        s_ref[a] = square
        eye = lax.broadcasted_iota(jnp.int32, (B, B), 0) == lax.broadcasted_iota(
            jnp.int32, (B, B), 1
        )
        m_ref[a] = (
            jnp.where(eye, weight, 0.0)
            + mix_ref[1] * own_ref[a].astype(jnp.float32)
            + mix_ref[2] * square.astype(jnp.float32)
        ).astype(jnp.bfloat16)


def product(block_cols, mixing, own, left, right):
    tile = jax.ShapeDtypeStruct(own.shape, own.dtype)
    vmem = pl.BlockSpec(memory_space=pltpu.VMEM)
    depth = len(right) * B
    return pl.pallas_call(
        product_kernel,
        out_shape=(tile, tile),
        in_specs=[pl.BlockSpec(memory_space=pltpu.SMEM)] * 2
        + [vmem]
        + [pl.BlockSpec(memory_space=pl.ANY)] * len(left)
        + [vmem] * len(right),
        out_specs=(vmem, vmem),
        scratch_shapes=[
            pltpu.VMEM((NC, len(right), B, B), jnp.bfloat16),
            pltpu.SemaphoreType.DMA((NC,)),
        ],
        cost_estimate=pl.CostEstimate(
            flops=2 * NC * B * depth * B, bytes_accessed=4 * NC * B * depth, transcendentals=0
        ),
        name="product",
    )(block_cols, mixing, own, *left, *right)


def solution(mesh):
    sizes = tuple(mesh.shape[a] for a in AXES)
    moves = {
        "za": lambda s: (s, 0, 0, 0),
        "zb": lambda s: (-s, 0, 0, 0),
        "xa": lambda s: (0, s, 0, 0),
        "xb": lambda s: (0, -s, 0, 0),
        "ya": lambda s: (0, 0, s, 0),
        "yb": lambda s: (0, 0, -s, 0),
        "core": lambda s: (0, 0, 0, 1),
    }
    perms = {k: permutation(sizes, m) for k, m in moves.items()}

    def send(value, name):
        return lax.ppermute(value, AXES, perms[name])

    def ring4(tile, axis):
        a1 = send(tile, axis + "a")
        b1 = send(tile, axis + "b")
        return [a1, b1, send(a1, axis + "a")]

    def panels(row_tile, col_tile):
        along_x = ring4(row_tile, "x")
        along_y = ring4(row_tile, "y")
        forward, backward = [col_tile], [col_tile]
        for _ in range(4):
            forward.append(send(forward[-1], "za"))
        for _ in range(3):
            backward.append(send(backward[-1], "zb"))
        own = forward + backward[1:]
        corners = ring4(jnp.concatenate([t[:PAIR] for t in along_x[:2]]), "y")
        corners += ring4(jnp.concatenate([t[PAIR:] for t in along_y[:2]]), "x")
        corners += ring4(along_x[2][:PAIR], "y")
        corners += ring4(along_y[2][PAIR:], "x")
        partner = [send(t, "core") for t in own]
        return [row_tile] + along_x + along_y + corners, own + partner

    def body(density, block_cols, mixing):
        own = density[:, 0]

        def step(_, tiles):
            return product(block_cols, mixing, own, *panels(*tiles))

        return lax.fori_loop(0, 2, step, (own, own))[0][:, None]

    in_specs = (P("row", ("col", "inner"), None, None), P(), P())
    out_specs = P("row", ("col", "inner"), None, None)
    return jax.shard_map(body, mesh=mesh, in_specs=in_specs, out_specs=out_specs, check_vma=False)
```

```python
import jax
import jax.numpy as jnp
from jax import lax
from jax.experimental import pallas as pl
from jax.experimental.pallas import tpu as pltpu
from jax.sharding import PartitionSpec as P


AXES = ("row", "col", "inner")
CORES = 2
NC = 4
B = 256
PIECES = (
    *(((0, 0),), ((-1, 0),), ((1, 0),), ((2, 0),), ((0, -1),), ((0, 1),), ((0, 2),)),
    *(((-1, -1), (1, -1)), ((-1, 1), (1, 1)), ((-1, -2), (1, -2))),
    *(((2, -1),), ((2, 1),), ((2, 2),)),
)
COLUMNS = (
    *((0, 0), (-1, 0), (-2, 0), (-3, 0), (-4, 0), (0, 1), (-1, 1), (-2, 1), (-3, 1)),
    *((1, 1), (2, 1), (3, 1), (4, 1), (1, 0), (2, 0), (3, 0)),
)
LEFTS = len(PIECES)
RIGHTS = len(COLUMNS)


def permutation(sizes, move):
    rows, cols, inners = sizes
    pairs = []
    for row in range(rows):
        for col in range(cols):
            for inner in range(inners):
                z, core = divmod(row, CORES)
                sign = 1 if core == 0 else -1
                dz, dx, dy, flip = move(sign)
                to_row = (z + dz) % (rows // CORES) * CORES + (core + flip) % CORES
                to = (to_row * cols + (col + dx) % cols) * inners + (inner + dy) % inners
                pairs.append(((row * cols + col) * inners + inner, to))
    return pairs


def product_kernel(*refs):
    cols_ref, mix_ref, own_ref = refs[:3]
    left, right = refs[3 : 3 + LEFTS], refs[3 + LEFTS : 3 + LEFTS + RIGHTS]
    s_ref, m_ref, lbuf, rbuf, lsem, rsem = refs[3 + LEFTS + RIGHTS :]
    row = lax.axis_index("row")
    x = lax.axis_index("col")
    y = lax.axis_index("inner")
    zs = lax.axis_size("row") // CORES
    xs = lax.axis_size("col")
    ys = lax.axis_size("inner")
    z = row // CORES
    core = row % CORES
    sign = 1 - 2 * core
    weight = jnp.where(row == x * ys + y, mix_ref[0], 0.0)

    def local(c, u):
        return cols_ref[c, u] - NC * u

    @pl.loop(0, NC)
    def _(c):
        a = local(c, row)
        for src, owners in zip(left, PIECES):
            for i, (first, second) in enumerate(owners):
                dx = jnp.where(core == 0, first, second)
                dy = jnp.where(core == 0, second, first)
                g = lax.rem(x + dx + xs, xs) * ys + lax.rem(y + dy + ys, ys)
                dst = lbuf.at[c, :, pl.ds(pl.multiple_of(g * B, B), B)]
                pltpu.make_async_copy(src.at[i * NC + a], dst, lsem.at[c]).start()
        for src, (hops, flip) in zip(right, COLUMNS):
            u = lax.rem(z + hops * sign + zs, zs) * CORES + (1 - core if flip else core)
            dst = rbuf.at[c, pl.ds(pl.multiple_of(u * B, B), B), :]
            pltpu.make_async_copy(src.at[local(c, u)], dst, rsem.at[c]).start()

    @pl.loop(0, NC)
    def _(c):
        pltpu.make_async_copy(lbuf.at[c], lbuf.at[c], lsem.at[c]).wait()
        pltpu.make_async_copy(rbuf.at[c], rbuf.at[c], rsem.at[c]).wait()
        a = local(c, row)
        total = jnp.dot(lbuf[c], rbuf[c], preferred_element_type=jnp.float32)
        square = total.astype(jnp.bfloat16)
        s_ref[a] = square
        eye = lax.broadcasted_iota(jnp.int32, (B, B), 0) == lax.broadcasted_iota(
            jnp.int32, (B, B), 1
        )
        m_ref[a] = (
            jnp.where(eye, weight, 0.0)
            + mix_ref[1] * own_ref[a].astype(jnp.float32)
            + mix_ref[2] * square.astype(jnp.float32)
        ).astype(jnp.bfloat16)


def product(block_cols, mixing, own, left, right):
    tile = jax.ShapeDtypeStruct(own.shape, own.dtype)
    vmem = pl.BlockSpec(memory_space=pltpu.VMEM)
    depth = len(right) * B
    return pl.pallas_call(
        product_kernel,
        out_shape=(tile, tile),
        in_specs=[pl.BlockSpec(memory_space=pltpu.SMEM)] * 2
        + [vmem]
        + [pl.BlockSpec(memory_space=pl.ANY)] * (len(left) + len(right)),
        out_specs=(vmem, vmem),
        scratch_shapes=[
            pltpu.VMEM((NC, B, depth), jnp.bfloat16),
            pltpu.VMEM((NC, depth, B), jnp.bfloat16),
            pltpu.SemaphoreType.DMA((NC,)),
            pltpu.SemaphoreType.DMA((NC,)),
        ],
        cost_estimate=pl.CostEstimate(
            flops=2 * NC * B * depth * B, bytes_accessed=4 * NC * B * depth, transcendentals=0
        ),
        name="product",
    )(block_cols, mixing, own, *left, *right)


def solution(mesh):
    sizes = tuple(mesh.shape[a] for a in AXES)
    moves = {
        "za": lambda s: (s, 0, 0, 0),
        "fa": lambda s: (0, 1, 0, 0) if s > 0 else (0, 0, 1, 0),
        "fb": lambda s: (0, -1, 0, 0) if s > 0 else (0, 0, -1, 0),
        "sa": lambda s: (0, 0, 1, 0) if s > 0 else (0, 1, 0, 0),
        "sb": lambda s: (0, 0, -1, 0) if s > 0 else (0, -1, 0, 0),
        "core": lambda s: (0, 0, 0, 1),
    }
    perms = {k: permutation(sizes, m) for k, m in moves.items()}

    def send(value, name):
        return lax.ppermute(value, AXES, perms[name])

    def panels(row_tile, col_tile):
        fa = send(row_tile, "fa")
        fb = send(row_tile, "fb")
        fc = send(fb, "fb")
        oa = send(row_tile, "sa")
        ob = send(row_tile, "sb")
        oc = send(ob, "sb")
        pair = jnp.concatenate([fa, fb])
        ra = send(pair, "sa")
        rb = send(pair, "sb")
        rc = send(ra, "sa")
        ga = send(fc, "sa")
        gb = send(fc, "sb")
        gc = send(gb, "sb")
        other = send(col_tile, "core")
        mine, theirs = [col_tile], [other]
        for _ in range(4):
            mine.append(send(mine[-1], "za"))
        for _ in range(3):
            theirs.append(send(theirs[-1], "za"))
        arrived = mine[1:] + theirs[1:]
        swapped = [send(t, "core") for t in arrived]
        left = [row_tile, fa, fb, fc, oa, ob, oc, ra, rb, rc, ga, gb, gc]
        return left, mine + theirs + swapped

    def body(density, block_cols, mixing):
        own = density[:, 0]

        def step(tiles):
            return product(block_cols, mixing, own, *panels(*tiles))

        return step(step((own, own)))[0][:, None]

    in_specs = (P("row", ("col", "inner"), None, None), P(), P())
    out_specs = P("row", ("col", "inner"), None, None)
    return jax.shard_map(body, mesh=mesh, in_specs=in_specs, out_specs=out_specs, check_vma=False)
```

```python
import jax
import jax.numpy as jnp
from jax import lax
from jax.experimental import pallas as pl
from jax.experimental.pallas import tpu as pltpu
from jax.sharding import PartitionSpec as P


AXES = ("row", "col", "inner")
CORES = 2
NC = 4
B = 256
PIECES = (
    *(((0, 0),), ((-1, 0),), ((1, 0),), ((2, 0),), ((0, -1),), ((0, 1),), ((0, 2),)),
    *(((-1, -1), (1, -1)), ((-1, 1), (1, 1)), ((-1, -2), (1, -2))),
    *(((2, -1),), ((2, 1),), ((2, 2),)),
)
COLUMNS = (
    *(((0, 0),), ((-1, 0),), ((-2, 0),), ((-3, 0),), ((-4, 0),)),
    *(((0, 1),), ((-1, 1),), ((-2, 1),), ((-3, 1),)),
    *(((1, 1), (1, 0), (2, 1), (2, 0)), ((3, 1), (3, 0), (4, 1))),
)
LEFTS = len(PIECES)
RIGHTS = len(COLUMNS)


def permutation(sizes, move):
    rows, cols, inners = sizes
    pairs = []
    for row in range(rows):
        for col in range(cols):
            for inner in range(inners):
                z, core = divmod(row, CORES)
                sign = 1 if core == 0 else -1
                dz, dx, dy, flip = move(sign)
                to_row = (z + dz) % (rows // CORES) * CORES + (core + flip) % CORES
                to = (to_row * cols + (col + dx) % cols) * inners + (inner + dy) % inners
                pairs.append(((row * cols + col) * inners + inner, to))
    return pairs


def product_kernel(*refs):
    cols_ref, mix_ref, own_ref = refs[:3]
    left, right = refs[3 : 3 + LEFTS], refs[3 + LEFTS : 3 + LEFTS + RIGHTS]
    s_ref, m_ref, lbuf, rbuf, lsem, rsem = refs[3 + LEFTS + RIGHTS :]
    row = lax.axis_index("row")
    x = lax.axis_index("col")
    y = lax.axis_index("inner")
    zs = lax.axis_size("row") // CORES
    xs = lax.axis_size("col")
    ys = lax.axis_size("inner")
    z = row // CORES
    core = row % CORES
    sign = 1 - 2 * core
    weight = jnp.where(row == x * ys + y, mix_ref[0], 0.0)

    def local(c, u):
        return cols_ref[c, u] - NC * u

    @pl.loop(0, NC)
    def _(c):
        a = local(c, row)
        for src, owners in zip(left, PIECES):
            for i, (first, second) in enumerate(owners):
                dx = jnp.where(core == 0, first, second)
                dy = jnp.where(core == 0, second, first)
                g = lax.rem(x + dx + xs, xs) * ys + lax.rem(y + dy + ys, ys)
                dst = lbuf.at[c, :, pl.ds(pl.multiple_of(g * B, B), B)]
                pltpu.make_async_copy(src.at[i * NC + a], dst, lsem.at[c]).start()
        for src, owners in zip(right, COLUMNS):
            for i, (hops, flip) in enumerate(owners):
                u = lax.rem(z + hops * sign + zs, zs) * CORES + (1 - core if flip else core)
                dst = rbuf.at[c, pl.ds(pl.multiple_of(u * B, B), B), :]
                pltpu.make_async_copy(src.at[i * NC + local(c, u)], dst, rsem.at[c]).start()

    @pl.loop(0, NC)
    def _(c):
        pltpu.make_async_copy(lbuf.at[c], lbuf.at[c], lsem.at[c]).wait()
        pltpu.make_async_copy(rbuf.at[c], rbuf.at[c], rsem.at[c]).wait()
        a = local(c, row)
        total = jnp.dot(lbuf[c], rbuf[c], preferred_element_type=jnp.float32)
        square = total.astype(jnp.bfloat16)
        s_ref[a] = square
        eye = lax.broadcasted_iota(jnp.int32, (B, B), 0) == lax.broadcasted_iota(
            jnp.int32, (B, B), 1
        )
        m_ref[a] = (
            jnp.where(eye, weight, 0.0)
            + mix_ref[1] * own_ref[a].astype(jnp.float32)
            + mix_ref[2] * square.astype(jnp.float32)
        ).astype(jnp.bfloat16)


def product(block_cols, mixing, own, left, right):
    tile = jax.ShapeDtypeStruct(own.shape, own.dtype)
    vmem = pl.BlockSpec(memory_space=pltpu.VMEM)
    depth = sum(len(owners) for owners in COLUMNS) * B
    return pl.pallas_call(
        product_kernel,
        out_shape=(tile, tile),
        in_specs=[pl.BlockSpec(memory_space=pltpu.SMEM)] * 2
        + [vmem]
        + [pl.BlockSpec(memory_space=pl.ANY)] * (len(left) + len(right)),
        out_specs=(vmem, vmem),
        scratch_shapes=[
            pltpu.VMEM((NC, B, depth), jnp.bfloat16),
            pltpu.VMEM((NC, depth, B), jnp.bfloat16),
            pltpu.SemaphoreType.DMA((NC,)),
            pltpu.SemaphoreType.DMA((NC,)),
        ],
        cost_estimate=pl.CostEstimate(
            flops=2 * NC * B * depth * B, bytes_accessed=4 * NC * B * depth, transcendentals=0
        ),
        name="product",
    )(block_cols, mixing, own, *left, *right)


def solution(mesh):
    sizes = tuple(mesh.shape[a] for a in AXES)
    moves = {
        "za": lambda s: (s, 0, 0, 0),
        "fa": lambda s: (0, 1, 0, 0) if s > 0 else (0, 0, 1, 0),
        "fb": lambda s: (0, -1, 0, 0) if s > 0 else (0, 0, -1, 0),
        "sa": lambda s: (0, 0, 1, 0) if s > 0 else (0, 1, 0, 0),
        "sb": lambda s: (0, 0, -1, 0) if s > 0 else (0, -1, 0, 0),
        "core": lambda s: (0, 0, 0, 1),
    }
    perms = {k: permutation(sizes, m) for k, m in moves.items()}

    def send(value, name):
        return lax.ppermute(value, AXES, perms[name])

    def panels(row_tile, col_tile):
        fa = send(row_tile, "fa")
        fb = send(row_tile, "fb")
        fc = send(fb, "fb")
        oa = send(row_tile, "sa")
        ob = send(row_tile, "sb")
        oc = send(ob, "sb")
        pair = jnp.concatenate([fa, fb])
        ra = send(pair, "sa")
        rb = send(pair, "sb")
        rc = send(ra, "sa")
        ga = send(fc, "sa")
        gb = send(fc, "sb")
        gc = send(gb, "sb")
        other = send(col_tile, "core")
        mine, theirs = [col_tile], [other]
        for _ in range(4):
            mine.append(send(mine[-1], "za"))
        for _ in range(3):
            theirs.append(send(theirs[-1], "za"))
        early = [t for pair in zip(mine[1:3], theirs[1:3]) for t in pair]
        arrived = [jnp.concatenate(early), jnp.concatenate([mine[3], theirs[3], mine[4]])]
        swapped = [send(t, "core") for t in arrived]
        left = [row_tile, fa, fb, fc, oa, ob, oc, ra, rb, rc, ga, gb, gc]
        return left, mine + theirs + swapped

    def body(density, block_cols, mixing):
        own = density[:, 0]

        def step(tiles):
            return product(block_cols, mixing, own, *panels(*tiles))

        return step(step((own, own)))[0][:, None]

    in_specs = (P("row", ("col", "inner"), None, None), P(), P())
    out_specs = P("row", ("col", "inner"), None, None)
    return jax.shard_map(body, mesh=mesh, in_specs=in_specs, out_specs=out_specs, check_vma=False)
```

```python
import functools

import jax
import jax.numpy as jnp
from jax import lax
from jax.experimental import pallas as pl
from jax.experimental.pallas import tpu as pltpu
from jax.sharding import PartitionSpec as P


AXES = ("row", "col", "inner")
CORES = 2
NC = 4
B = 256
PIECES = (
    *(((0, 0),), ((-1, 0),), ((1, 0),), ((2, 0),), ((0, -1),), ((0, 1),), ((0, 2),)),
    *(((-1, -1), (1, -1)), ((-1, 1), (1, 1)), ((-1, -2), (1, -2))),
    *(((2, -1),), ((2, 1),), ((2, 2),)),
)
COLUMNS = (
    *(((0, 0),), ((-1, 0),), ((-2, 0),), ((-3, 0),), ((-4, 0),)),
    *(((0, 1),), ((-1, 1),), ((-2, 1),), ((-3, 1),)),
    *(((1, 1), (1, 0), (2, 1), (2, 0)), ((3, 1), (3, 0), (4, 1))),
)
LEFTS = len(PIECES)
RIGHTS = len(COLUMNS)


def permutation(sizes, move):
    rows, cols, inners = sizes
    pairs = []
    for row in range(rows):
        for col in range(cols):
            for inner in range(inners):
                z, core = divmod(row, CORES)
                sign = 1 if core == 0 else -1
                dz, dx, dy, flip = move(sign)
                to_row = (z + dz) % (rows // CORES) * CORES + (core + flip) % CORES
                to = (to_row * cols + (col + dx) % cols) * inners + (inner + dy) % inners
                pairs.append(((row * cols + col) * inners + inner, to))
    return pairs


def product_kernel(last, *refs):
    cols_ref, mix_ref, own_ref = refs[:3]
    left, right = refs[3 : 3 + LEFTS], refs[3 + LEFTS : 3 + LEFTS + RIGHTS]
    s_ref, *m_refs, lbuf, rbuf, lsem, rsem = refs[3 + LEFTS + RIGHTS :]
    row = lax.axis_index("row")
    x = lax.axis_index("col")
    y = lax.axis_index("inner")
    zs = lax.axis_size("row") // CORES
    xs = lax.axis_size("col")
    ys = lax.axis_size("inner")
    z = row // CORES
    core = row % CORES
    sign = 1 - 2 * core
    weight = jnp.where(row == x * ys + y, mix_ref[0], 0.0)

    def local(c, u):
        return cols_ref[c, u] - NC * u

    @pl.loop(0, NC)
    def _(c):
        a = local(c, row)
        for src, owners in zip(left, PIECES):
            for i, (first, second) in enumerate(owners):
                dx = jnp.where(core == 0, first, second)
                dy = jnp.where(core == 0, second, first)
                g = lax.rem(x + dx + xs, xs) * ys + lax.rem(y + dy + ys, ys)
                dst = lbuf.at[c, :, pl.ds(pl.multiple_of(g * B, B), B)]
                pltpu.make_async_copy(src.at[i * NC + a], dst, lsem.at[c]).start()
        for src, owners in zip(right, COLUMNS):
            for i, (hops, flip) in enumerate(owners):
                u = lax.rem(z + hops * sign + zs, zs) * CORES + (1 - core if flip else core)
                dst = rbuf.at[c, pl.ds(pl.multiple_of(u * B, B), B), :]
                pltpu.make_async_copy(src.at[i * NC + local(c, u)], dst, rsem.at[c]).start()

    @pl.loop(0, NC)
    def _(c):
        pltpu.make_async_copy(lbuf.at[c], lbuf.at[c], lsem.at[c]).wait()
        pltpu.make_async_copy(rbuf.at[c], rbuf.at[c], rsem.at[c]).wait()
        a = local(c, row)
        total = jnp.dot(lbuf[c], rbuf[c], preferred_element_type=jnp.float32)
        square = total.astype(jnp.bfloat16)
        s_ref[a] = square
        if last:
            return
        eye = lax.broadcasted_iota(jnp.int32, (B, B), 0) == lax.broadcasted_iota(
            jnp.int32, (B, B), 1
        )
        m_refs[0][a] = (
            jnp.where(eye, weight, 0.0)
            + mix_ref[1] * own_ref[a].astype(jnp.float32)
            + mix_ref[2] * square.astype(jnp.float32)
        ).astype(jnp.bfloat16)


def product(last, block_cols, mixing, own, left, right):
    tile = jax.ShapeDtypeStruct(own.shape, own.dtype)
    vmem = pl.BlockSpec(memory_space=pltpu.VMEM)
    depth = sum(len(owners) for owners in COLUMNS) * B
    return pl.pallas_call(
        functools.partial(product_kernel, last),
        out_shape=(tile,) if last else (tile, tile),
        in_specs=[pl.BlockSpec(memory_space=pltpu.SMEM)] * 2
        + [vmem]
        + [pl.BlockSpec(memory_space=pl.ANY)] * (len(left) + len(right)),
        out_specs=(vmem,) if last else (vmem, vmem),
        scratch_shapes=[
            pltpu.VMEM((NC, B, depth), jnp.bfloat16),
            pltpu.VMEM((NC, depth, B), jnp.bfloat16),
            pltpu.SemaphoreType.DMA((NC,)),
            pltpu.SemaphoreType.DMA((NC,)),
        ],
        cost_estimate=pl.CostEstimate(
            flops=2 * NC * B * depth * B, bytes_accessed=4 * NC * B * depth, transcendentals=0
        ),
        name="product",
    )(block_cols, mixing, own, *left, *right)


def solution(mesh):
    sizes = tuple(mesh.shape[a] for a in AXES)
    moves = {
        "za": lambda s: (s, 0, 0, 0),
        "fa": lambda s: (0, 1, 0, 0) if s > 0 else (0, 0, 1, 0),
        "fb": lambda s: (0, -1, 0, 0) if s > 0 else (0, 0, -1, 0),
        "sa": lambda s: (0, 0, 1, 0) if s > 0 else (0, 1, 0, 0),
        "sb": lambda s: (0, 0, -1, 0) if s > 0 else (0, -1, 0, 0),
        "core": lambda s: (0, 0, 0, 1),
    }
    perms = {k: permutation(sizes, m) for k, m in moves.items()}

    def send(value, name):
        return lax.ppermute(value, AXES, perms[name])

    def panels(row_tile, col_tile):
        fa = send(row_tile, "fa")
        fb = send(row_tile, "fb")
        fc = send(fb, "fb")
        oa = send(row_tile, "sa")
        ob = send(row_tile, "sb")
        oc = send(ob, "sb")
        pair = jnp.concatenate([fa, fb])
        ra = send(pair, "sa")
        rb = send(pair, "sb")
        rc = send(ra, "sa")
        ga = send(fc, "sa")
        gb = send(fc, "sb")
        gc = send(gb, "sb")
        other = send(col_tile, "core")
        mine, theirs = [col_tile], [other]
        for _ in range(4):
            mine.append(send(mine[-1], "za"))
        for _ in range(3):
            theirs.append(send(theirs[-1], "za"))
        early = [t for pair in zip(mine[1:3], theirs[1:3]) for t in pair]
        arrived = [jnp.concatenate(early), jnp.concatenate([mine[3], theirs[3], mine[4]])]
        swapped = [send(t, "core") for t in arrived]
        left = [row_tile, fa, fb, fc, oa, ob, oc, ra, rb, rc, ga, gb, gc]
        return left, mine + theirs + swapped

    def body(density, block_cols, mixing):
        own = density[:, 0]

        def step(n, tiles):
            return product(n == 1, block_cols, mixing, own, *panels(*tiles))

        return step(1, step(0, (own, own)))[0][:, None]

    in_specs = (P("row", ("col", "inner"), None, None), P(), P())
    out_specs = P("row", ("col", "inner"), None, None)
    return jax.shard_map(body, mesh=mesh, in_specs=in_specs, out_specs=out_specs, check_vma=False)
```
